32 devices in a mesh: group: 8 (over z, core), member: 4 (over y, x).
Axes of the slice: x: 2, y: 2, z: 4, core: 2. Of those that a mesh axis runs over, the one named last changes fastest.
Arguments:
- media: bfloat16 [160, 256, 1024], P(('group', 'member')), may hold values from -6 to 6
- latents: bfloat16 [160, 64, 1024], P(('group', 'member')), may hold values from -6 to 6
- cotangent: bfloat16 [160, 64, 1024], P(('group', 'member')), may hold values from -6 to 6
- image_counts: int32 [32], P(('group', 'member')), may hold values from 1 to 5
- media_gain: bfloat16 [1024], P('member'), may hold values from 0.099609375 to 1.8984375
- media_bias: bfloat16 [1024], P('member'), may hold values from -3 to 3
- latent_gain: bfloat16 [1024], P('member'), may hold values from 0.099609375 to 1.8984375
- latent_bias: bfloat16 [1024], P('member'), may hold values from -3 to 3
- ff_gain: bfloat16 [1024], P('member'), may hold values from 0.099609375 to 1.8984375
- ff_bias: bfloat16 [1024], P('member'), may hold values from -3 to 3
- w_query: bfloat16 [1024, 512], P('member'), may hold values from -0.1875 to 0.1875
- w_keyval: bfloat16 [1024, 1024], P('member'), may hold values from -0.1875 to 0.1875
- w_out: bfloat16 [512, 1024], P('member'), may hold values from -1.5 to 1.5
- w_hidden: bfloat16 [1024, 4096], P('member'), may hold values from -0.1875 to 0.1875
- w_back: bfloat16 [4096, 1024], P('member'), may hold values from -0.09375 to 0.09375
Outputs:
- latent_out: bfloat16 [160, 64, 1024], P(('group', 'member'))
- media_grad: bfloat16 [160, 256, 1024], P(('group', 'member'))
- latent_grad: bfloat16 [160, 64, 1024], P(('group', 'member'))
- grad_media_gain: float32 [1024], P('member')
- grad_media_bias: float32 [1024], P('member')
- grad_latent_gain: float32 [1024], P('member')
- grad_latent_bias: float32 [1024], P('member')
- grad_ff_gain: float32 [1024], P('member')
- grad_ff_bias: float32 [1024], P('member')
- grad_w_query: float32 [1024, 512], P('member')
- grad_w_keyval: float32 [1024, 1024], P('member')
- grad_w_out: float32 [512, 1024], P('member')
- grad_w_hidden: float32 [1024, 4096], P('member')
- grad_w_back: float32 [4096, 1024], P('member')
The draws below stay inside these ranges and needn't reach their ends.
All inputs are finite; a program needn't handle non-finite values.
Results may differ from the reference program's by a relative error of at most 0.019.
Values may be sent and summed in bfloat16 or wider, within the bound.
No kernel may reach another device: no remote copies, remote signals or barrier semaphores. Data moves between devices by JAX's collectives and lax.ppermute only.
A program may use at most 192 MiB of HBM per device.

```python
import jax
import jax.numpy as jnp
from jax import lax

D = 1024
HEADS = 8
HEAD_DIM = 64
FF = 4096
LATENTS = 64
MEDIA = 256
SLOT_SAMPLE = 5
INNER = 512
SLOTS_DEV = 5
SAMPLES = 32
IMAGES = 160


def place_ends(array, rng, smallest, largest):
    longest = array.shape.index(max(array.shape))
    spots = []
    for shift in (0, 1):
        where = [jax.random.randint(jax.random.fold_in(rng, axis), (), 0, length) for axis, length in enumerate(array.shape)]
        where[longest] = (where[longest] + shift) % array.shape[longest]
        spots.append(tuple(where))
    return array.at[spots[0]].set(smallest).at[spots[1]].set(largest)


def shard_levels(key, extent, cuts, least, largest):
    factor_of, own = 1.0, jax.random.fold_in(key, 6)
    for dim, shards_of in cuts:
        steps = jnp.exp(jax.random.uniform(jax.random.fold_in(own, dim), (shards_of,), jnp.float32, least / len(cuts), largest / len(cuts)))
        factor_of = factor_of * jnp.repeat(steps, extent[dim] // shards_of).reshape([-1 if axis == dim else 1 for axis in range(len(extent))])
    return factor_of


def centred(stream_key, shape, scale, reach, shards=(), kind=jnp.bfloat16):
    values = scale * jax.random.normal(stream_key, shape, jnp.float32)
    if shards:
        values = values * shard_levels(stream_key, shape, shards, -0.22, 0.18)
    return jnp.clip(values, -reach, reach).astype(kind)


def setup_inputs(seed: int = 0) -> dict:
    key_list = jax.random.split(jax.random.key(seed), 16)
    return {
        "media": centred(key_list[0], (IMAGES, MEDIA, D), 1.0, 6.0, ((0, 32),)),
        "latents": centred(key_list[1], (IMAGES, LATENTS, D), 1.0, 6.0, ((0, 32),)),
        "cotangent": centred(key_list[2], (IMAGES, LATENTS, D), 1.0, 6.0, ((0, 32),)),
        "image_counts": place_ends(jax.random.randint(key_list[3], (SAMPLES,), 1, SLOT_SAMPLE + 1), jax.random.fold_in(key_list[3], 1), 1, SLOT_SAMPLE).astype(jnp.int32),
        "media_gain": jnp.clip(1.0 + 0.18 * jax.random.normal(key_list[4], (D,), jnp.float32), 0.099609375, 1.8984375).astype(jnp.bfloat16),
        "media_bias": centred(key_list[5], (D,), 0.5, 3.0, ((0, 4),)),
        "latent_gain": jnp.clip(1.0 + 0.18 * jax.random.normal(key_list[6], (D,), jnp.float32), 0.099609375, 1.8984375).astype(jnp.bfloat16),
        "latent_bias": centred(key_list[7], (D,), 0.5, 3.0, ((0, 4),)),
        "ff_gain": jnp.clip(1.0 + 0.18 * jax.random.normal(key_list[8], (D,), jnp.float32), 0.099609375, 1.8984375).astype(jnp.bfloat16),
        "ff_bias": centred(key_list[9], (D,), 0.5, 3.0, ((0, 4),)),
        "w_query": centred(key_list[10], (D, INNER), D ** -0.5, 0.1875, ((0, 4),)),
        "w_keyval": centred(key_list[11], (D, 2 * INNER), D ** -0.5, 0.1875, ((0, 4),)),
        "w_out": centred(key_list[12], (INNER, D), (INNER // 32) ** -0.5, 1.5, ((0, 4),)),
        "w_hidden": centred(key_list[13], (D, FF), D ** -0.5, 0.1875, ((0, 4),)),
        "w_back": centred(key_list[14], (FF, D), FF ** -0.5, 0.09375, ((0, 4),)),
    }


@jax.custom_vjp
def low(v):
    return lax.optimization_barrier(v.astype(jnp.bfloat16)).astype(jnp.float32)

@jax.custom_vjp
def low_back(v):
    return v

def low_keep(v):
    return (low(v), None)

def low_pass(kept, grad):
    return (grad,)

def back_keep(v):
    return (v, None)

def back_low(kept, grad):
    return (low(grad),)
low.defvjp(low_keep, low_pass)
low_back.defvjp(back_keep, back_low)
EPSILON = 1e-05

def norm_rows(values, gain, shift):
    center = values - lax.optimization_barrier(jnp.mean(values, axis=-1, keepdims=True))
    spread = lax.optimization_barrier(jnp.mean(center * center, axis=-1, keepdims=True))
    return center * lax.rsqrt(spread + EPSILON) * gain + shift

def project(left, weight):
    return jnp.einsum('bnd,de->bne', left, weight, precision=lax.Precision.HIGHEST)

def layer(weights, media_f, latent_f):
    media_gain, media_bias, latent_gain, latent_bias, ff_gain, ff_bias, w_query, w_keyval, w_out, w_hidden, w_back = weights
    batch = latent_f.shape[0]
    scale = 1.0 / HEAD_DIM ** 0.5
    media_norm = low(norm_rows(media_f, media_gain, media_bias))
    latent_norm = low(norm_rows(latent_f, latent_gain, latent_bias))
    query = low(low_back(project(latent_norm, w_query)))
    joined = jnp.concatenate([media_norm, latent_norm], axis=1)
    keyval = low(low_back(project(joined, w_keyval)))
    keys = keyval[..., :INNER].reshape(batch, MEDIA + LATENTS, HEADS, HEAD_DIM)
    values = keyval[..., INNER:].reshape(batch, MEDIA + LATENTS, HEADS, HEAD_DIM)
    heads_q = query.reshape(batch, LATENTS, HEADS, HEAD_DIM)
    scores = low_back(jnp.einsum('blhe,bkhe->bhlk', heads_q, keys, precision=lax.Precision.HIGHEST) * scale)
    top = lax.optimization_barrier(jnp.max(scores, axis=-1, keepdims=True))
    expo = jnp.exp(scores - top)
    probs = low(expo / lax.optimization_barrier(jnp.sum(expo, axis=-1, keepdims=True)))
    mixed = jnp.einsum('bhlk,bkhe->blhe', probs, values, precision=lax.Precision.HIGHEST).reshape(batch, LATENTS, INNER)
    mixed = low(low_back(mixed))
    middle = latent_f + low_back(project(mixed, w_out))
    ff_norm = low(norm_rows(middle, ff_gain, ff_bias))
    hidden = low_back(project(ff_norm, w_hidden))
    active = low(jax.nn.gelu(hidden, approximate=False))
    return middle + low_back(project(active, w_back))

def reference(media, latents, cotangent, image_counts, media_gain, media_bias, latent_gain, latent_bias, ff_gain, ff_bias, w_query, w_keyval, w_out, w_hidden, w_back):
    weights = tuple((p.astype(jnp.float32) for p in (media_gain, media_bias, latent_gain, latent_bias, ff_gain, ff_bias, w_query, w_keyval, w_out, w_hidden, w_back)))
    slot_index = jnp.arange(IMAGES, dtype=jnp.int32)
    live = (slot_index % SLOT_SAMPLE < jnp.repeat(image_counts, SLOT_SAMPLE)).astype(jnp.float32)
    blocks = IMAGES // SLOTS_DEV

    def whole(params, media_f, latent_f):

        def one_block(pair):
            return layer(params, pair[0], pair[1])
        result = lax.map(jax.checkpoint(one_block), (media_f.reshape(blocks, SLOTS_DEV, MEDIA, D), latent_f.reshape(blocks, SLOTS_DEV, LATENTS, D)))
        return result.reshape(IMAGES, LATENTS, D) * live[:, None, None]
    result, pullback = jax.vjp(whole, weights, media.astype(jnp.float32), latents.astype(jnp.float32))
    grads, media_grad, latent_grad = pullback(cotangent.astype(jnp.float32))
    return (result.astype(jnp.bfloat16), media_grad.astype(jnp.bfloat16), latent_grad.astype(jnp.bfloat16), grads[0], grads[1], grads[2], grads[3], grads[4], grads[5], grads[6], grads[7], grads[8], grads[9], grads[10])
```

```python
import jax
import jax.numpy as jnp
from jax import lax
from jax.sharding import Mesh
from jax.sharding import PartitionSpec as P

HEADS = 8
HEAD_DIM = 64
SLOT_SAMPLE = 5
EPSILON = 1e-05

F32 = jnp.float32
BF16 = jnp.bfloat16
SWAP = [(0, 1), (1, 0)]
MEMBER = ("my", "mx")
EVERY = ("z", "core", "my", "mx")


def after(value, *others):
    return lax.optimization_barrier((value, *others))[0]


def low(v):
    return v.astype(BF16)


def swap_core(v):
    return lax.ppermute(v, "core", SWAP)


class Fast:
    def __init__(self):
        self.me = lax.axis_index("my") * 2 + lax.axis_index("mx")
        self.count = 4

    def of(self, rel):
        return self.me ^ rel

    def gather(self, v):
        half = v.shape[0] // 2
        from_x = lax.ppermute(v, "mx", SWAP)
        from_y = lax.ppermute(v, "my", SWAP)
        top = lax.ppermute(from_x[:half], "my", SWAP)
        bottom = lax.ppermute(from_y[half:], "mx", SWAP)
        return [v, from_x, from_y, jnp.concatenate([top, bottom], 0)]

    def exchange(self, parts):
        corner = [(0, 3), (1, 2), (2, 1), (3, 0)]
        return [
            parts[0],
            lax.ppermute(parts[1], "mx", SWAP),
            lax.ppermute(parts[2], "my", SWAP),
            lax.ppermute(parts[3], MEMBER, corner),
        ]

    def scatter(self, parts):
        half = parts[0].shape[0] // 2
        f = [p.astype(F32) for p in parts]
        ax = lax.ppermute(low(jnp.stack([parts[1][:half], parts[3][:half]])), "mx", SWAP)
        by = lax.ppermute(low(jnp.stack([parts[2][half:], parts[3][half:]])), "my", SWAP)
        a2 = lax.ppermute(low(f[2][:half] + ax[1].astype(F32)), "my", SWAP)
        b2 = lax.ppermute(low(f[1][half:] + by[1].astype(F32)), "mx", SWAP)
        return jnp.concatenate(
            [
                f[0][:half] + ax[0].astype(F32) + a2.astype(F32),
                f[0][half:] + by[0].astype(F32) + b2.astype(F32),
            ],
            0,
        )

    def small_sum(self, v):
        v = v + lax.ppermute(v, "mx", SWAP)
        return v + lax.ppermute(v, "my", SWAP)


class Wide:
    def __init__(self, count):
        self.me = lax.axis_index(MEMBER)
        self.count = count

    def of(self, rel):
        return rel

    def gather(self, v):
        full = lax.all_gather(v, MEMBER, axis=0, tiled=False)
        return [full[i] for i in range(self.count)]

    def exchange(self, parts):
        full = lax.all_to_all(jnp.stack(parts), MEMBER, 0, 0, tiled=False)
        return [full[i] for i in range(self.count)]

    def scatter(self, parts):
        full = low(jnp.stack(parts))
        return lax.psum_scatter(full, MEMBER, scatter_dimension=0, tiled=False).astype(F32)

    def small_sum(self, v):
        return lax.psum(v, MEMBER)


def sum_z(v, nz):
    if nz != 4:
        return low(lax.psum(low(v).astype(F32), "z"))
    place = lax.axis_index("z")
    first = lax.ppermute(low(v), "z", [(0, 1), (3, 2)])
    pair = low(v + first.astype(F32))
    second = lax.ppermute(pair, "z", [(1, 2), (2, 1)])
    total = low(pair.astype(F32) + second.astype(F32))
    third = lax.ppermute(total, "z", [(1, 0), (2, 3)])
    outer = (place == 0) | (place == 3)
    return jnp.where(outer, third, total)


def small_sum_z(v, nz):
    if nz != 4:
        return lax.psum(v, "z")
    v = v + lax.ppermute(v, "z", [(0, 1), (1, 0), (2, 3), (3, 2)])
    return v + lax.ppermute(v, "z", [(0, 2), (2, 0), (1, 3), (3, 1)])


def norm_stats(values):
    center = values - jnp.mean(values, axis=-1, keepdims=True)
    spread = jnp.mean(center * center, axis=-1, keepdims=True)
    inv = lax.rsqrt(spread + EPSILON)
    return center * inv, inv


def norm_back(grad, normed, inv, gain):
    u = grad * gain
    mean_u = jnp.mean(u, axis=-1, keepdims=True)
    mean_un = jnp.mean(u * normed, axis=-1, keepdims=True)
    return (u - mean_u - normed * mean_un) * inv


def dot(a, b, dims):
    return lax.dot_general(a, b, (dims, ((), ())), preferred_element_type=F32)


def gelu_parts(v):
    cdf = 0.5 * (1.0 + lax.erf(v * (0.5**0.5)))
    pdf = jnp.exp(-0.5 * v * v) * 0.3989422804014327
    return v * cdf, cdf + v * pdf


def in_order(net, parts):
    stacked = jnp.stack(parts)
    return jnp.stack(
        [lax.dynamic_index_in_dim(stacked, net.of(a), 0, keepdims=False) for a in range(net.count)]
    )


def build(nz, members):
    def shards(
        media,
        latents,
        cotangent,
        image_counts,
        media_gain,
        media_bias,
        latent_gain,
        latent_bias,
        ff_gain,
        ff_bias,
        w_query,
        w_keyval,
        w_out,
        w_hidden,
        w_back,
    ):
        net = Fast() if members == 4 else Wide(members)
        core = lax.axis_index("core")
        slots, n_media, width = media.shape
        n_lat = latents.shape[1]
        n_all = n_media + n_lat
        inner = w_query.shape[1]
        rows = slots * n_lat
        scale = 1.0 / HEAD_DIM**0.5
        ff_own = w_back.shape[0]

        vec = jnp.stack([media_gain, media_bias, latent_gain, latent_bias, ff_gain, ff_bias])
        vec = jnp.concatenate([vec, jnp.zeros((2, vec.shape[1]), BF16)], 0)
        if members == 4:
            vecs = net.exchange([vec] * 4)
        else:
            vecs = net.gather(vec)
        vec_all = in_order(net, vecs).astype(F32)
        vec_all = jnp.swapaxes(vec_all, 0, 1).reshape(8, width)
        mg, mb, lg, lb, fg, fb = (vec_all[i] for i in range(6))

        def whole(w, dep):
            own = w.shape[0]
            half = lax.dynamic_slice_in_dim(w, core * (own // 2), own // 2, 0)
            if dep is not None:
                half = after(half, dep)
            parts = net.gather(half)
            mine = jnp.stack(parts)
            other = swap_core(mine)
            pair = jnp.where(core == 0, jnp.stack([mine, other], 1), jnp.stack([other, mine], 1))
            pair = [pair[i].reshape(w.shape) for i in range(net.count)]
            return in_order(net, pair).reshape(net.count * own, w.shape[1]), parts[1]

        wkv, dep = whole(w_keyval, None)
        wq, dep_q = whole(w_query, dep)
        wo, dep_o = whole(w_out, dep)

        half_ff = ff_own // 2
        sends = [
            lax.dynamic_slice_in_dim(w_hidden, net.of(r) * ff_own + core * half_ff, half_ff, 1)
            for r in range(net.count)
        ]
        sends = list(lax.optimization_barrier((*sends, dep_q, dep_o)))[: net.count]
        got = jnp.stack(net.exchange(sends))
        got_other = swap_core(got)
        wh = jnp.where(
            core == 0,
            jnp.concatenate([got, got_other], 2),
            jnp.concatenate([got_other, got], 2),
        )
        wh = in_order(net, [wh[i] for i in range(net.count)]).reshape(width, ff_own)

        position = lax.broadcasted_iota(jnp.int32, (slots // SLOT_SAMPLE, SLOT_SAMPLE), 1)
        live = (position < image_counts[:, None]).reshape(slots, 1, 1).astype(F32)
        g_out = cotangent.astype(F32) * live
        g_low = low(g_out).reshape(rows, width)
        g_parts = net.gather(after(g_low, got))

        media_f = media.astype(F32)
        latent_f = latents.astype(F32)
        media_n, media_inv = norm_stats(media_f)
        latent_n, latent_inv = norm_stats(latent_f)
        joined = jnp.concatenate([low(media_n * mg + mb), low(latent_n * lg + lb)], 1)
        latent_norm = joined[:, n_media:]
        query = low(dot(latent_norm, wq, ((2,), (0,))))
        keyval = low(dot(joined, wkv, ((2,), (0,))))
        keys = keyval[..., :inner].reshape(slots, n_all, HEADS, HEAD_DIM)
        values = keyval[..., inner:].reshape(slots, n_all, HEADS, HEAD_DIM)
        heads_q = query.reshape(slots, n_lat, HEADS, HEAD_DIM)

        def ein(spec, a, b):
            return jnp.einsum(spec, a, b, preferred_element_type=F32)

        scores = ein("blhe,bkhe->bhlk", heads_q, keys) * scale
        top = jnp.max(scores, axis=-1, keepdims=True)
        expo = jnp.exp(scores - top)
        probs_f = expo / jnp.sum(expo, axis=-1, keepdims=True)
        probs = low(probs_f)
        mixed = low(ein("bhlk,bkhe->blhe", probs, values).reshape(slots, n_lat, inner))
        middle = latent_f + dot(mixed, wo, ((2,), (0,)))
        mid_n, mid_inv = norm_stats(middle)
        ff_norm = low(mid_n * fg + fb).reshape(rows, width)

        x_all = jnp.concatenate(net.gather(ff_norm), 0)
        g_all = jnp.concatenate(g_parts, 0)
        hidden = dot(x_all, wh, ((1,), (0,)))
        act, slope = gelu_parts(hidden)
        act = low(act)
        g_act = dot(g_all, w_back, ((1,), (1,)))
        g_hid = low(g_act * slope)
        g_ff = low(dot(g_hid, wh, ((1,), (1,))))
        g_ffnorm = net.scatter([g_ff[i * rows : (i + 1) * rows] for i in range(net.count)])
        out = low(dot(act, w_back, ((1,), (0,))))
        out = after(out, g_ffnorm)
        out = net.scatter([out[i * rows : (i + 1) * rows] for i in range(net.count)])
        latent_out = low((middle + out.reshape(slots, n_lat, width)) * live)

        gwb = dot(act, g_all, ((0,), (0,)))
        gwb_pair = gwb.reshape(2, half_ff, width)
        keep = lax.dynamic_index_in_dim(gwb_pair, core, 0, keepdims=False)
        send = low(lax.dynamic_index_in_dim(gwb_pair, 1 - core, 0, keepdims=False))
        gwb_sum = sum_z(keep + swap_core(send).astype(F32), nz)
        gwh = dot(x_all, g_hid, ((0,), (0,)))
        keep = lax.dynamic_slice_in_dim(gwh, core * half_ff, half_ff, 1)
        send = low(lax.dynamic_slice_in_dim(gwh, (1 - core) * half_ff, half_ff, 1))
        gwh_half = low(keep + swap_core(send).astype(F32))
        gwh_half = gwh_half.reshape(net.count, width // net.count, half_ff)
        gwh_parts = net.exchange(
            [
                lax.dynamic_index_in_dim(gwh_half, net.of(r), 0, keepdims=False)
                for r in range(net.count)
            ]
        )
        gwh_sum = sum_z(jnp.stack(gwh_parts).astype(F32), nz)

        g_ffn = g_ffnorm.reshape(slots, n_lat, width)
        g_middle = g_out + norm_back(g_ffn, mid_n, mid_inv, fg)
        mid_low = low(g_middle)
        g_mixed = low(dot(mid_low, wo, ((2,), (1,)))).reshape(slots, n_lat, HEADS, HEAD_DIM)
        g_values = ein("bhlk,blhe->bkhe", probs, g_mixed)
        g_probs = ein("blhe,bkhe->bhlk", g_mixed, values)
        g_scores = low(
            probs_f * (g_probs - jnp.sum(probs_f * g_probs, axis=-1, keepdims=True))
        )
        g_query = low(
            (ein("bhlk,bkhe->blhe", g_scores, keys) * scale).reshape(slots, n_lat, inner)
        )
        g_keys = ein("bhlk,blhe->bkhe", g_scores, heads_q) * scale
        g_keyval = low(
            jnp.concatenate(
                [g_keys.reshape(slots, n_all, inner), g_values.reshape(slots, n_all, inner)], -1
            )
        )
        gwkv = dot(joined, g_keyval, ((0, 1), (0, 1)))
        gwq = dot(latent_norm, g_query, ((0, 1), (0, 1)))
        gwo = dot(mixed, mid_low, ((0, 1), (0, 1)))

        def pack(kv, q, o):
            n = net.count
            kv = kv.reshape(n, 2, width // n // 2, width)
            q = q.reshape(n, 2, width // n // 2, inner)
            o = o.reshape(n, 2, inner // n // 2, width)
            cut = q.shape[2] // 2
            q = jnp.concatenate([q[:, :, :cut], q[:, :, cut:]], 3)
            return jnp.concatenate([kv, q, o], 2)

        packed = pack(gwkv, gwq, gwo)
        keep = lax.dynamic_index_in_dim(packed, core, 1, keepdims=False)
        send = low(lax.dynamic_index_in_dim(packed, 1 - core, 1, keepdims=False))
        half_sum = keep + swap_core(send).astype(F32)
        attn = net.scatter(
            [
                lax.dynamic_index_in_dim(half_sum, net.of(r), 0, keepdims=False)
                for r in range(net.count)
            ]
        )
        attn = sum_z(attn, nz)

        g_joined = dot(g_keyval, wkv, ((2,), (1,)))
        g_med = g_joined[:, :n_media]
        g_lat = dot(g_query, wq, ((2,), (1,))) + g_joined[:, n_media:]
        media_grad = low(norm_back(g_med, media_n, media_inv, mg))
        latent_grad = low(g_middle + norm_back(g_lat, latent_n, latent_inv, lg))
        small = jnp.stack(
            [
                jnp.sum(g_med * media_n, (0, 1)),
                jnp.sum(g_med, (0, 1)),
                jnp.sum(g_lat * latent_n, (0, 1)),
                jnp.sum(g_lat, (0, 1)),
                jnp.sum(g_ffn * mid_n, (0, 1)),
                jnp.sum(g_ffn, (0, 1)),
            ]
        )
        small = jnp.concatenate([small, jnp.zeros((2, width), F32)], 0)
        small = small + swap_core(small)
        small = small_sum_z(net.small_sum(small), nz)
        mine = lax.axis_index(MEMBER)
        small = lax.dynamic_slice_in_dim(small, mine * (width // net.count), width // net.count, 1)

        def join(v, axis):
            o = swap_core(v)
            return jnp.where(
                core == 0, jnp.concatenate([v, o], axis), jnp.concatenate([o, v], axis)
            ).astype(F32)

        n = net.count
        kv_rows, q_rows, o_rows = width // n // 2, width // n // 4, inner // n // 2
        kv = join(attn[:kv_rows], 0)
        q = attn[kv_rows : kv_rows + q_rows]
        q = join(jnp.concatenate([q[:, :inner], q[:, inner:]], 0), 0)
        o = join(attn[kv_rows + q_rows :], 0)
        wb_out = join(gwb_sum, 0)
        wh_out = join(gwh_sum, 2)
        wh_out = in_order(net, [wh_out[i] for i in range(n)])
        wh_out = jnp.swapaxes(wh_out, 0, 1).reshape(width // n, n * ff_own)
        return (
            latent_out,
            media_grad,
            latent_grad,
            *(small[i] for i in range(6)),
            q,
            kv,
            o,
            wh_out,
            wb_out,
        )

    return shards


def solution(mesh):
    groups, members = mesh.shape["group"], mesh.shape["member"]
    nz = groups // 2
    side = 2 if members == 4 else 1
    cut = Mesh(mesh.devices.reshape(nz, 2, side, members // side), EVERY)
    rows3 = P(EVERY, None, None)
    in_specs = (rows3,) * 3 + (P(EVERY),) + (P(MEMBER),) * 6 + (P(MEMBER, None),) * 5
    out_specs = (rows3,) * 3 + (P(MEMBER),) * 6 + (P(MEMBER, None),) * 5
    return jax.shard_map(
        build(nz, members), mesh=cut, in_specs=in_specs, out_specs=out_specs, check_vma=False
    )
```

```python
import jax
import jax.numpy as jnp
from jax import lax
from jax.sharding import Mesh
from jax.sharding import PartitionSpec as P

HEADS = 8
HEAD_DIM = 64
SLOT_SAMPLE = 5
EPSILON = 1e-05

F32 = jnp.float32
BF16 = jnp.bfloat16
SWAP = [(0, 1), (1, 0)]
MEMBER = ("my", "mx")
EVERY = ("z", "core", "my", "mx")


def after(value, *others):
    return lax.optimization_barrier((value, *others))[0]


def low(v):
    return v.astype(BF16)


def swap_core(v):
    return lax.ppermute(v, "core", SWAP)


class Fast:
    def __init__(self):
        self.me = lax.axis_index("my") * 2 + lax.axis_index("mx")
        self.count = 4

    def of(self, rel):
        return self.me ^ rel

    def gather(self, v):
        half = v.shape[0] // 2
        from_x = lax.ppermute(v, "mx", SWAP)
        from_y = lax.ppermute(v, "my", SWAP)
        top = lax.ppermute(from_x[:half], "my", SWAP)
        bottom = lax.ppermute(from_y[half:], "mx", SWAP)
        return [v, from_x, from_y, jnp.concatenate([top, bottom], 0)]

    def exchange(self, parts):
        corner = [(0, 3), (1, 2), (2, 1), (3, 0)]
        return [
            parts[0],
            lax.ppermute(parts[1], "mx", SWAP),
            lax.ppermute(parts[2], "my", SWAP),
            lax.ppermute(parts[3], MEMBER, corner),
        ]

    def scatter(self, parts, *late):
        half = parts[0].shape[0] // 2
        f = [p.astype(F32) for p in parts]
        ax = lax.ppermute(low(jnp.stack([parts[1][:half], parts[3][:half]])), "mx", SWAP)
        by = lax.ppermute(low(jnp.stack([parts[2][half:], parts[3][half:]])), "my", SWAP)
        if late:
            ax, by = lax.optimization_barrier((ax, by, *late))[:2]
        a2 = lax.ppermute(low(f[2][:half] + ax[1].astype(F32)), "my", SWAP)
        b2 = lax.ppermute(low(f[1][half:] + by[1].astype(F32)), "mx", SWAP)
        return jnp.concatenate(
            [
                f[0][:half] + ax[0].astype(F32) + a2.astype(F32),
                f[0][half:] + by[0].astype(F32) + b2.astype(F32),
            ],
            0,
        )

    def small_sum(self, v):
        v = v + lax.ppermute(v, "mx", SWAP)
        return v + lax.ppermute(v, "my", SWAP)


class Wide:
    def __init__(self, count):
        self.me = lax.axis_index(MEMBER)
        self.count = count

    def of(self, rel):
        return rel

    def gather(self, v):
        full = lax.all_gather(v, MEMBER, axis=0, tiled=False)
        return [full[i] for i in range(self.count)]

    def exchange(self, parts):
        full = lax.all_to_all(jnp.stack(parts), MEMBER, 0, 0, tiled=False)
        return [full[i] for i in range(self.count)]

    def scatter(self, parts, *late):
        full = low(jnp.stack(parts))
        return lax.psum_scatter(full, MEMBER, scatter_dimension=0, tiled=False).astype(F32)

    def small_sum(self, v):
        return lax.psum(v, MEMBER)


class SumZ:
    def __init__(self, v, nz):
        self.nz = nz
        self.value = v
        if nz == 4:
            self.first = lax.ppermute(low(v), "z", [(0, 1), (3, 2)])

    def middle(self, *deps):
        if self.nz == 4:
            pair = low(self.value + after(self.first, *deps).astype(F32))
            self.value = pair
            self.second = lax.ppermute(pair, "z", [(1, 2), (2, 1)])

    def last(self, *deps):
        if self.nz != 4:
            self.third = self.total = low(lax.psum(low(self.value).astype(F32), "z"))
        else:
            self.total = low(self.value.astype(F32) + after(self.second, *deps).astype(F32))
            self.third = lax.ppermute(self.total, "z", [(1, 0), (2, 3)])

    def done(self):
        place = lax.axis_index("z")
        outer = (place == 0) | (place == self.nz - 1)
        return jnp.where(outer, self.third, self.total)


def norm_stats(values):
    center = values - jnp.mean(values, axis=-1, keepdims=True)
    spread = jnp.mean(center * center, axis=-1, keepdims=True)
    inv = lax.rsqrt(spread + EPSILON)
    return center * inv, inv


def norm_back(grad, normed, inv, gain):
    u = grad * gain
    mean_u = jnp.mean(u, axis=-1, keepdims=True)
    mean_un = jnp.mean(u * normed, axis=-1, keepdims=True)
    return (u - mean_u - normed * mean_un) * inv


def dot(a, b, dims):
    return lax.dot_general(a, b, (dims, ((), ())), preferred_element_type=F32)


def gelu_parts(v):
    cdf = 0.5 * (1.0 + lax.erf(v * (0.5**0.5)))
    pdf = jnp.exp(-0.5 * v * v) * 0.3989422804014327
    return v * cdf, cdf + v * pdf


def in_order(net, parts):
    stacked = jnp.stack(parts)
    return jnp.stack(
        [lax.dynamic_index_in_dim(stacked, net.of(a), 0, keepdims=False) for a in range(net.count)]
    )


def build(nz, members):
    def shards(
        media,
        latents,
        cotangent,
        image_counts,
        media_gain,
        media_bias,
        latent_gain,
        latent_bias,
        ff_gain,
        ff_bias,
        w_query,
        w_keyval,
        w_out,
        w_hidden,
        w_back,
    ):
        net = Fast() if members == 4 else Wide(members)
        core = lax.axis_index("core")
        slots, n_media, width = media.shape
        n_lat = latents.shape[1]
        n_all = n_media + n_lat
        inner = w_query.shape[1]
        rows = slots * n_lat
        scale = 1.0 / HEAD_DIM**0.5
        ff_own = w_back.shape[0]

        vec = jnp.stack([media_gain, media_bias, latent_gain, latent_bias, ff_gain, ff_bias])
        vec = jnp.concatenate([vec, jnp.zeros((2, vec.shape[1]), BF16)], 0)
        if members == 4:
            vecs = net.exchange([vec] * 4)
        else:
            vecs = net.gather(vec)
        vec_all = in_order(net, vecs).astype(F32)
        vec_all = jnp.swapaxes(vec_all, 0, 1).reshape(8, width)
        mg, mb, lg, lb, fg, fb = (vec_all[i] for i in range(6))

        def half_of(w):
            own = w.shape[0] // 2
            return lax.dynamic_slice_in_dim(w, core * own, own, 0)

        n = net.count
        kv_rows, q_rows, o_rows = width // n // 2, width // n // 4, inner // n // 2
        half_q = half_of(w_query)
        pack_w = jnp.concatenate(
            [half_of(w_keyval), jnp.concatenate([half_q[:q_rows], half_q[q_rows:]], 1), half_of(w_out)], 0
        )
        mine = jnp.stack(net.gather(after(pack_w, *vecs)))
        other = swap_core(mine)
        pair = jnp.where(core == 0, jnp.stack([mine, other], 1), jnp.stack([other, mine], 1))
        pair = in_order(net, [pair[i] for i in range(n)])
        wkv = pair[:, :, :kv_rows].reshape(width, width)
        wq = pair[:, :, kv_rows : kv_rows + q_rows]
        wq = jnp.concatenate([wq[..., :inner], wq[..., inner:]], 2).reshape(width, inner)
        wo = pair[:, :, kv_rows + q_rows :].reshape(inner, width)

        half_ff = ff_own // 2
        sends = [
            lax.dynamic_slice_in_dim(w_hidden, net.of(r) * ff_own + core * half_ff, half_ff, 1)
            for r in range(net.count)
        ]
        sends = list(lax.optimization_barrier((*sends, mine)))[: net.count]
        got = jnp.stack(net.exchange(sends))
        got_other = swap_core(got)
        wh = jnp.where(
            core == 0,
            jnp.concatenate([got, got_other], 2),
            jnp.concatenate([got_other, got], 2),
        )
        wh = in_order(net, [wh[i] for i in range(net.count)]).reshape(width, ff_own)

        position = lax.broadcasted_iota(jnp.int32, (slots // SLOT_SAMPLE, SLOT_SAMPLE), 1)
        live = (position < image_counts[:, None]).reshape(slots, 1, 1).astype(F32)
        g_out = cotangent.astype(F32) * live
        g_low = low(g_out).reshape(rows, width)
        g_parts = net.gather(after(g_low, got))

        media_f = media.astype(F32)
        latent_f = latents.astype(F32)
        media_n, media_inv = norm_stats(media_f)
        latent_n, latent_inv = norm_stats(latent_f)
        joined = jnp.concatenate([low(media_n * mg + mb), low(latent_n * lg + lb)], 1)
        latent_norm = joined[:, n_media:]
        query = low(dot(latent_norm, wq, ((2,), (0,))))
        keyval = low(dot(joined, wkv, ((2,), (0,))))
        keys = keyval[..., :inner].reshape(slots, n_all, HEADS, HEAD_DIM)
        values = keyval[..., inner:].reshape(slots, n_all, HEADS, HEAD_DIM)
        heads_q = query.reshape(slots, n_lat, HEADS, HEAD_DIM)

        def ein(spec, a, b):
            return jnp.einsum(spec, a, b, preferred_element_type=F32)

        scores = ein("blhe,bkhe->bhlk", heads_q, keys) * scale
        top = jnp.max(scores, axis=-1, keepdims=True)
        expo = jnp.exp(scores - top)
        probs_f = expo / jnp.sum(expo, axis=-1, keepdims=True)
        probs = low(probs_f)
        mixed = low(ein("bhlk,bkhe->blhe", probs, values).reshape(slots, n_lat, inner))
        middle = latent_f + dot(mixed, wo, ((2,), (0,)))
        mid_n, mid_inv = norm_stats(middle)
        ff_norm = low(mid_n * fg + fb).reshape(rows, width)

        x_all = jnp.concatenate(net.gather(ff_norm), 0)
        g_all = jnp.concatenate(g_parts, 0)
        hidden = dot(x_all, wh, ((1,), (0,)))
        act, slope = gelu_parts(hidden)
        act = low(act)
        g_act = dot(g_all, w_back, ((1,), (1,)))
        g_hid = low(g_act * slope)
        g_ff = low(dot(g_hid, wh, ((1,), (1,))))
        gwb = dot(act, g_all, ((0,), (0,)))
        gwb_pair = gwb.reshape(2, half_ff, width)
        keep_b = lax.dynamic_index_in_dim(gwb_pair, core, 0, keepdims=False)
        send_b = swap_core(low(lax.dynamic_index_in_dim(gwb_pair, 1 - core, 0, keepdims=False)))
        g_ff = after(g_ff, send_b)
        g_ffnorm = net.scatter([g_ff[i * rows : (i + 1) * rows] for i in range(n)])
        z_b = SumZ(keep_b + send_b.astype(F32), nz)
        gwh = dot(x_all, g_hid, ((0,), (0,)))
        keep = lax.dynamic_slice_in_dim(gwh, core * half_ff, half_ff, 1)
        send = low(lax.dynamic_slice_in_dim(gwh, (1 - core) * half_ff, half_ff, 1))
        gwh_half = low(keep + swap_core(send).astype(F32))
        gwh_half = after(gwh_half, g_ffnorm).reshape(n, width // n, half_ff)
        gwh_parts = jnp.stack(
            net.exchange(
                [lax.dynamic_index_in_dim(gwh_half, net.of(r), 0, keepdims=False) for r in range(n)]
            )
        )
        out = low(dot(act, w_back, ((1,), (0,))))

        g_ffn = g_ffnorm.reshape(slots, n_lat, width)
        g_middle = g_out + norm_back(g_ffn, mid_n, mid_inv, fg)
        mid_low = low(g_middle)
        g_mixed = low(dot(mid_low, wo, ((2,), (1,)))).reshape(slots, n_lat, HEADS, HEAD_DIM)
        g_values = ein("bhlk,blhe->bkhe", probs, g_mixed)
        g_probs = ein("blhe,bkhe->bhlk", g_mixed, values)
        g_scores = low(
            probs_f * (g_probs - jnp.sum(probs_f * g_probs, axis=-1, keepdims=True))
        )
        g_scores, gwh_parts = lax.optimization_barrier((g_scores, gwh_parts))
        z_b.middle(g_scores)
        z_h = SumZ(gwh_parts.astype(F32), nz)
        g_query = low(
            (ein("bhlk,bkhe->blhe", g_scores, keys) * scale).reshape(slots, n_lat, inner)
        )
        g_keys = ein("bhlk,blhe->bkhe", g_scores, heads_q) * scale
        g_keyval = low(
            jnp.concatenate(
                [g_keys.reshape(slots, n_all, inner), g_values.reshape(slots, n_all, inner)], -1
            )
        )
        gwkv = dot(joined, g_keyval, ((0, 1), (0, 1)))
        gwq = dot(latent_norm, g_query, ((0, 1), (0, 1)))
        gwo = dot(mixed, mid_low, ((0, 1), (0, 1)))

        def pack(kv, q, o):
            kv = kv.reshape(n, 2, kv_rows, width)
            q = q.reshape(n, 2, 2 * q_rows, inner)
            o = o.reshape(n, 2, o_rows, width)
            q = jnp.concatenate([q[:, :, :q_rows], q[:, :, q_rows:]], 3)
            return jnp.concatenate([kv, q, o], 2)

        packed = pack(gwkv, gwq, gwo)
        keep = lax.dynamic_index_in_dim(packed, core, 1, keepdims=False)
        send = low(lax.dynamic_index_in_dim(packed, 1 - core, 1, keepdims=False))
        send = swap_core(send)
        half_sum = keep + send.astype(F32)
        attn = net.scatter(
            [lax.dynamic_index_in_dim(half_sum, net.of(r), 0, keepdims=False) for r in range(n)]
        )
        z_b.last(send)
        z_h.middle(z_b.third if nz != 4 else z_b.total)

        g_joined = dot(after(g_keyval, send), wkv, ((2,), (1,)))
        g_med = g_joined[:, :n_media]
        g_lat = dot(g_query, wq, ((2,), (1,))) + g_joined[:, n_media:]
        media_grad = low(norm_back(g_med, media_n, media_inv, mg))
        latent_grad = low(g_middle + norm_back(g_lat, latent_n, latent_inv, lg))
        small = jnp.stack(
            [
                jnp.sum(g_med * media_n, (0, 1)),
                jnp.sum(g_med, (0, 1)),
                jnp.sum(g_lat * latent_n, (0, 1)),
                jnp.sum(g_lat, (0, 1)),
                jnp.sum(g_ffn * mid_n, (0, 1)),
                jnp.sum(g_ffn, (0, 1)),
            ]
        )
        small = jnp.concatenate([small, jnp.zeros((2, width), F32)], 0)
        small = net.small_sum(small + swap_core(small))
        spot = lax.axis_index(MEMBER) * 2 + core
        cut = width // n // 2
        small = lax.dynamic_slice_in_dim(small, spot * cut, cut, 1)
        extra = small.reshape(8 * cut // 128, 128)
        tail = attn.shape[0]
        flat = jnp.zeros((16, width), F32).at[: extra.shape[0], :128].set(extra)
        z_a = SumZ(jnp.concatenate([attn, flat], 0), nz)
        z_h.last(media_grad)
        z_a.middle()
        z_a.last()
        attn = z_a.done()
        out = after(out, g_keyval)
        out = net.scatter([out[i * rows : (i + 1) * rows] for i in range(n)], media_grad)
        latent_out = low((middle + out.reshape(slots, n_lat, width)) * live)
        gwb_sum, gwh_sum = z_b.done(), z_h.done()

        def join(v, axis):
            o = swap_core(v)
            return jnp.where(
                core == 0, jnp.concatenate([v, o], axis), jnp.concatenate([o, v], axis)
            ).astype(F32)

        small = join(attn[tail : tail + 8 * cut // 128, :128].reshape(8, cut), 1)
        kv = join(attn[:kv_rows], 0)
        q = attn[kv_rows : kv_rows + q_rows]
        q = join(jnp.concatenate([q[:, :inner], q[:, inner:]], 0), 0)
        o = join(attn[kv_rows + q_rows : tail], 0)
        wb_out = join(gwb_sum, 0)
        wh_out = join(gwh_sum, 2)
        wh_out = in_order(net, [wh_out[i] for i in range(n)])
        wh_out = jnp.swapaxes(wh_out, 0, 1).reshape(width // n, n * ff_own)
        return (
            latent_out,
            media_grad,
            latent_grad,
            *(small[i] for i in range(6)),
            q,
            kv,
            o,
            wh_out,
            wb_out,
        )

    return shards


def solution(mesh):
    groups, members = mesh.shape["group"], mesh.shape["member"]
    nz = groups // 2
    side = 2 if members == 4 else 1
    cut = Mesh(mesh.devices.reshape(nz, 2, side, members // side), EVERY)
    rows3 = P(EVERY, None, None)
    in_specs = (rows3,) * 3 + (P(EVERY),) + (P(MEMBER),) * 6 + (P(MEMBER, None),) * 5
    out_specs = (rows3,) * 3 + (P(MEMBER),) * 6 + (P(MEMBER, None),) * 5
    return jax.shard_map(
        build(nz, members), mesh=cut, in_specs=in_specs, out_specs=out_specs, check_vma=False
    )
```
